32 devices in a mesh: fsdp: 32 (over z, y, x, core).
Axes of the slice: x: 2, y: 2, z: 4, core: 2. Of those that a mesh axis runs over, the one named last changes fastest.
Arguments:
- tokens: bfloat16 [8192, 768], P('fsdp'), may hold values from -6 to 6
- cotangent: bfloat16 [8192, 768], P('fsdp'), may hold values from -6 to 6
- segment_ids: int32 [8192], P('fsdp'), may hold values from 0 to 29, as said below
- weight_qkv: float32 [768, 2304], P('fsdp'), may hold values from -0.21875 to 0.21875
- weight_dense: float32 [768, 768], P('fsdp'), may hold values from -1.75 to 1.75
- weight_up: float32 [768, 3072], P('fsdp'), may hold values from -0.21875 to 0.21875
- weight_down: float32 [3072, 768], P('fsdp'), may hold values from -0.109375 to 0.109375
- vectors: float32 [9984], P('fsdp'), may hold values from -0.5 to 1.5
- first_qkv: float32 [768, 2304], P('fsdp'), may hold values from -0.001953125 to 0.001953125
- first_dense: float32 [768, 768], P('fsdp'), may hold values from -0.001953125 to 0.001953125
- first_up: float32 [768, 3072], P('fsdp'), may hold values from -0.001953125 to 0.001953125
- first_down: float32 [3072, 768], P('fsdp'), may hold values from -0.001953125 to 0.001953125
- first_vectors: float32 [9984], P('fsdp'), may hold values from -0.001953125 to 0.001953125
- second_qkv: float32 [768, 2304], P('fsdp'), may hold values from 6.103516e-08 to 2.4414064e-07
- second_dense: float32 [768, 768], P('fsdp'), may hold values from 5.493164e-07 to 2.1972655e-06
- second_up: float32 [768, 3072], P('fsdp'), may hold values from 6.1035157e-06 to 2.4414063e-05
- second_down: float32 [3072, 768], P('fsdp'), may hold values from 1.5258789e-06 to 6.1035157e-06
- second_vectors: float32 [9984], P('fsdp'), may hold values from 6.1035156e-06 to 0.00048828125
Outputs:
- block_out: bfloat16 [8192, 768], P('fsdp')
- grad_tokens: float32 [8192, 768], P('fsdp')
- grad_qkv: float32 [768, 2304], P('fsdp')
- grad_dense: float32 [768, 768], P('fsdp')
- grad_up: float32 [768, 3072], P('fsdp')
- grad_down: float32 [3072, 768], P('fsdp')
- grad_vectors: float32 [9984], P('fsdp')
- new_qkv: float32 [768, 2304], P('fsdp')
- new_dense: float32 [768, 768], P('fsdp')
- new_up: float32 [768, 3072], P('fsdp')
- new_down: float32 [3072, 768], P('fsdp')
- new_vectors: float32 [9984], P('fsdp')
- new_first_qkv: float32 [768, 2304], P('fsdp')
- new_first_dense: float32 [768, 768], P('fsdp')
- new_first_up: float32 [768, 3072], P('fsdp')
- new_first_down: float32 [3072, 768], P('fsdp')
- new_first_vectors: float32 [9984], P('fsdp')
- new_second_qkv: float32 [768, 2304], P('fsdp')
- new_second_dense: float32 [768, 768], P('fsdp')
- new_second_up: float32 [768, 3072], P('fsdp')
- new_second_down: float32 [3072, 768], P('fsdp')
- new_second_vectors: float32 [9984], P('fsdp')
The draws below stay inside these ranges and needn't reach their ends.
Inputs may be any that keep to these rules, and one draw needn't show every extreme that they name: `segment_ids`: never falling along the tokens, starting at 0 and rising by one at each new document; every document holds 1 to 1024 tokens, one exactly 1024; no document begins at a positive multiple of 256; every device from index 4 on holds exactly one document start.
All inputs are finite; a program needn't handle non-finite values.
Results may differ from the reference program's by a relative error of at most 0.006.
The reference program's roundings to bfloat16 on the way count: a program that leaves them out, or rounds other values in their place, can miss the bound.
Values may be sent and summed in bfloat16 or wider, within the bound.
No kernel may reach another device: no remote copies, remote signals or barrier semaphores. Data moves between devices by JAX's collectives and lax.ppermute only.
A program may use at most 192 MiB of HBM per device.

```python
import math
import jax
import jax.numpy as jnp
from jax import lax

D = 768
HEADS = 12
HEAD_DIM = 64
ROTARY = 16
FF = 3072
SEQ = 1024
TOK_DEV = 256
TOKENS = 8192
SEQUENCES = 8
VECTOR_LEN = 9984


def draw_segment_ids(key, part):
    device_count = TOKENS // TOK_DEV
    stride = SEQ // TOK_DEV
    first_key, second_key = jax.random.split(jax.random.fold_in(key, 71), 2)
    common_offset = jax.random.randint(first_key, (), 1, TOK_DEV)
    offsets = jax.random.randint(second_key, (device_count,), 1, TOK_DEV)
    device_ids = jnp.arange(device_count)
    forced = device_ids % stride == 0
    present = (device_ids == 0) | (device_ids >= stride)
    offsets = jnp.where(forced, common_offset, offsets)
    flags = jnp.zeros((TOKENS,), jnp.int32).at[device_ids * TOK_DEV + offsets].set(present.astype(jnp.int32))
    return jnp.cumsum(flags).astype(jnp.int32)


def draw_vectors(key, part):
    spread = jax.random.uniform(key, (9 * D + FF,), jnp.float32, -1.0, 1.0)
    places = jnp.arange(9 * D + FF)
    is_gain = (places < D) | (places >= 2 * D) & (places < 3 * D)
    return jnp.where(is_gain, 1.0 + 0.5 * spread, 0.5 * spread)


def draw_second_vectors(key, part):
    unit = jax.random.uniform(jax.random.fold_in(key, 29), (9 * D + FF,), jnp.float32, 0.0, 1.0)
    places = jnp.arange(9 * D + FF)
    settled = (places >= D) & (places < 2 * D) | (places >= 6 * D) & (places < 7 * D)
    lower = jnp.where(settled, jnp.float32(0.05), jnp.float32(1.0)) / jnp.float32(TOKENS)
    return lower * jnp.exp(unit * jnp.log(jnp.float32(4.0)))


def level_of(key, extent, shards, smallest, high):
    def one(axis_at, parts):
        draws = jax.random.uniform(jax.random.fold_in(jax.random.fold_in(key, 6), axis_at), (parts,), jnp.float32, smallest / len(shards), high / len(shards))
        return jnp.repeat(jnp.exp(draws), extent[axis_at] // parts).reshape((-1,) + (1,) * (len(extent) - axis_at - 1))

    level = one(*shards[0])
    for cut in shards[1:]:
        level = level * one(*cut)
    return level


def centred(stream_key, extent, width, limit, cuts=(), kind=jnp.bfloat16):
    array = width * jax.random.normal(stream_key, extent, jnp.float32)
    if cuts:
        array = array * level_of(stream_key, extent, cuts, -0.22, 0.18)
    return jnp.clip(array, -limit, limit).astype(kind)


def setup_inputs(seed: int = 0) -> dict:
    key_of = jax.random.split(jax.random.key(seed), 19)
    tokens = centred(key_of[0], (TOKENS, D), 1.0, 6.0, ((0, 32),))
    cotangent = centred(key_of[1], (TOKENS, D), 1.0, 6.0, ((0, 32),))
    segment_ids = draw_segment_ids(jax.random.fold_in(key_of[18], 71), 0)
    weight_qkv = centred(key_of[3], (D, 3 * D), D ** -0.5, 0.21875, ((0, 32),), jnp.float32)
    weight_dense = centred(key_of[4], (D, D), (D // 64) ** -0.5, 1.75, ((0, 32),), jnp.float32)
    weight_up = centred(key_of[5], (D, FF), D ** -0.5, 0.21875, ((0, 32),), jnp.float32)
    weight_down = centred(key_of[6], (FF, D), FF ** -0.5, 0.109375, ((0, 32),), jnp.float32)
    vectors = draw_vectors(jax.random.fold_in(key_of[18], 71), 0)
    first_qkv = centred(key_of[8], (D, 3 * D), (0.03 / TOKENS ** 0.5), 0.001953125, ((0, 32),), jnp.float32)
    first_dense = centred(key_of[9], (D, D), (0.03 / TOKENS ** 0.5), 0.001953125, ((0, 32),), jnp.float32)
    first_up = centred(key_of[10], (D, FF), (0.03 / TOKENS ** 0.5), 0.001953125, ((0, 32),), jnp.float32)
    first_down = centred(key_of[11], (FF, D), (0.03 / TOKENS ** 0.5), 0.001953125, ((0, 32),), jnp.float32)
    first_vectors = centred(key_of[12], (VECTOR_LEN,), (0.03 / TOKENS ** 0.5), 0.001953125, ((0, 32),), jnp.float32)
    second_qkv = jnp.clip(jnp.exp(math.log(2.4414063659605745e-07) - 1.3862944 * jax.random.uniform(key_of[13], (D, 3 * D), jnp.float32) ** level_of(key_of[13], (D, 3 * D), ((0, 32),), -0.2, 0.2)), 6.103515914901436e-08, 2.4414063659605745e-07)
    second_dense = jnp.clip(jnp.exp(math.log(2.197265530412551e-06) - 1.3862944 * jax.random.uniform(key_of[14], (D, D), jnp.float32) ** level_of(key_of[14], (D, D), ((0, 32),), -0.2, 0.2)), 5.493163826031378e-07, 2.197265530412551e-06)
    second_up = jnp.clip(jnp.exp(math.log(2.441406286379788e-05) - 1.3862944 * jax.random.uniform(key_of[15], (D, FF), jnp.float32) ** level_of(key_of[15], (D, FF), ((0, 32),), -0.2, 0.2)), 6.10351571594947e-06, 2.441406286379788e-05)
    second_down = jnp.clip(jnp.exp(math.log(6.10351571594947e-06) - 1.3862944 * jax.random.uniform(key_of[16], (FF, D), jnp.float32) ** level_of(key_of[16], (FF, D), ((0, 32),), -0.2, 0.2)), 1.5258789289873675e-06, 6.10351571594947e-06)
    second_vectors = draw_second_vectors(jax.random.fold_in(key_of[18], 71), 0)
    return {"tokens": tokens, "cotangent": cotangent, "segment_ids": segment_ids, "weight_qkv": weight_qkv, "weight_dense": weight_dense, "weight_up": weight_up, "weight_down": weight_down, "vectors": vectors, "first_qkv": first_qkv, "first_dense": first_dense, "first_up": first_up, "first_down": first_down, "first_vectors": first_vectors, "second_qkv": second_qkv, "second_dense": second_dense, "second_up": second_up, "second_down": second_down, "second_vectors": second_vectors}


epsilon = 1e-05
rate_matrix = 0.05
rate_vector = 0.3
beta_one = 0.9
beta_two = 0.95
weight_decay = 0.01
adam_steps = 5
adam_floor = 1e-08
masked_score = -1e+30
erf_scale = 0.7071067811865476
normal_density = 0.3989422804014327

def layer_norm(inputs):
    center = lax.optimization_barrier(jnp.mean(inputs, axis=-1, keepdims=True))
    offset = inputs - center
    variance = lax.optimization_barrier(jnp.mean(offset * offset, axis=-1, keepdims=True))
    scale_inv = lax.rsqrt(variance + epsilon)
    return (offset * scale_inv, scale_inv)

def norm_backward(upstream, normed, scale_inv, norm_gain):
    scaled = upstream * norm_gain
    projected = scaled - lax.optimization_barrier(jnp.mean(scaled, axis=-1, keepdims=True)) - normed * lax.optimization_barrier(jnp.mean(scaled * normed, axis=-1, keepdims=True))
    return (scale_inv * projected, lax.optimization_barrier(jnp.sum(upstream * normed, axis=0)), lax.optimization_barrier(jnp.sum(upstream, axis=0)))

def gelu_exact(values):
    return 0.5 * values * (1.0 + jax.scipy.special.erf(values * erf_scale))

def gelu_slope(values):
    return 0.5 * (1.0 + jax.scipy.special.erf(values * erf_scale)) + values * jnp.exp(-0.5 * values * values) * normal_density

def rotary_tables(phase):
    half_dims = jnp.arange(ROTARY // 2).astype(jnp.float32)
    frequency = jnp.exp(half_dims * (-2.0 * jnp.log(jnp.float32(10000.0)) / ROTARY))
    angles = phase[:, None] * frequency[None, :]
    return (jnp.cos(angles)[:, None, :], jnp.sin(angles)[:, None, :])

def rotate(values, cos_table, sin_table):
    low_half = values[..., :ROTARY // 2]
    high_half = values[..., ROTARY // 2:ROTARY]
    return jnp.concatenate([low_half * cos_table - high_half * sin_table, high_half * cos_table + low_half * sin_table, values[..., ROTARY:]], axis=-1)

def unrotate(gradient, cos_table, sin_table):
    low_half = gradient[..., :ROTARY // 2]
    high_half = gradient[..., ROTARY // 2:ROTARY]
    return jnp.concatenate([low_half * cos_table + high_half * sin_table, high_half * cos_table - low_half * sin_table, gradient[..., ROTARY:]], axis=-1)

def split_vectors(packed_vec):
    bounds = [0, D, 2 * D, 3 * D, 4 * D, 7 * D, 8 * D, 8 * D + FF, 9 * D + FF]
    return [packed_vec[bounds[member]:bounds[member + 1]] for member in range(8)]

def attention_forward(queries, key_vecs, value_vecs, allowed):
    scores = jnp.einsum('qhd,khd->hqk', queries.astype(jnp.float32), key_vecs.astype(jnp.float32)) * 0.125
    scores = jnp.where(allowed[None], scores, masked_score)
    highest = lax.optimization_barrier(jnp.max(scores, axis=-1, keepdims=True))
    log_total = highest + jnp.log(lax.optimization_barrier(jnp.sum(jnp.exp(scores - highest), axis=-1, keepdims=True)))
    prob_half = jnp.exp(scores - log_total).astype(jnp.bfloat16)
    mixed = jnp.einsum('hqk,khd->qhd', prob_half.astype(jnp.float32), value_vecs.astype(jnp.float32)).astype(jnp.bfloat16)
    return (mixed, log_total)

def attention_backward(queries, key_vecs, value_vecs, allowed, mixed, log_total, grad_mixed):
    scores = jnp.einsum('qhd,khd->hqk', queries.astype(jnp.float32), key_vecs.astype(jnp.float32)) * 0.125
    scores = jnp.where(allowed[None], scores, masked_score)
    prob_exact = jnp.exp(scores - log_total)
    prob_half = prob_exact.astype(jnp.bfloat16)
    upstream = grad_mixed.astype(jnp.float32)
    prob_grad = jnp.einsum('qhd,khd->hqk', upstream, value_vecs.astype(jnp.float32))
    row_inner = jnp.transpose(lax.optimization_barrier(jnp.sum(upstream * mixed.astype(jnp.float32), axis=-1)))[:, :, None]
    score_grad = (prob_exact * (prob_grad - row_inner)).astype(jnp.bfloat16).astype(jnp.float32)
    grad_query = jnp.einsum('hqk,khd->qhd', score_grad, key_vecs.astype(jnp.float32)) * 0.125
    grad_key = jnp.einsum('hqk,qhd->khd', score_grad, queries.astype(jnp.float32)) * 0.125
    grad_value = jnp.einsum('hqk,qhd->khd', prob_half.astype(jnp.float32), upstream)
    return (grad_query, grad_key, grad_value)

def prepare(tokens16, pieces):
    inputs = tokens16.astype(jnp.float32)
    normed, scale_inv = layer_norm(inputs)
    input_one = (normed * pieces[0] + pieces[1]).astype(jnp.bfloat16)
    input_two = (normed * pieces[2] + pieces[3]).astype(jnp.bfloat16)
    return (inputs, normed, scale_inv, input_one, input_two)

def adamw_update(master, moment_one, moment_two, gradient, rate):
    moment_one = beta_one * moment_one + (1.0 - beta_one) * gradient
    moment_two = beta_two * moment_two + (1.0 - beta_two) * gradient * gradient
    corrected = moment_one / (1.0 - beta_one ** adam_steps) / (jnp.sqrt(moment_two / (1.0 - beta_two ** adam_steps)) + adam_floor)
    return (master - rate * (corrected + weight_decay * master), moment_one, moment_two)

def reference(tokens, cotangent, segment_ids, weight_qkv, weight_dense, weight_up, weight_down, vectors, first_qkv, first_dense, first_up, first_down, first_vectors, second_qkv, second_dense, second_up, second_down, second_vectors):
    masters = (weight_qkv, weight_dense, weight_up, weight_down, vectors)
    mat_qkv, mat_dense, mat_up, mat_down = tuple((master.astype(jnp.bfloat16) for master in masters[:4]))
    pieces = split_vectors(lax.optimization_barrier(vectors.astype(jnp.bfloat16)).astype(jnp.float32))
    gain_one, bias_one, gain_two, bias_two, bias_qkv, bias_dense, bias_up, bias_down = pieces
    positions = jnp.arange(TOKENS, dtype=jnp.int32)
    doc_first = jnp.searchsorted(segment_ids, segment_ids, side='left').astype(jnp.int32)
    phase = (positions - doc_first).astype(jnp.float32)
    tok_blocks = tokens.reshape(SEQUENCES, SEQ, D)
    up_blocks = cotangent.reshape(SEQUENCES, SEQ, D)
    phase_blocks = phase.reshape(SEQUENCES, SEQ)
    start_blocks = doc_first.reshape(SEQUENCES, SEQ)
    block_ids = jnp.arange(SEQUENCES, dtype=jnp.int32)

    def front(inputs):
        tokens16, phase_rows = inputs
        _, _, _, input_one, _ = prepare(tokens16, pieces)
        qkv = jnp.dot(input_one, mat_qkv, preferred_element_type=jnp.float32) + bias_qkv
        cos_table, sin_table = rotary_tables(phase_rows)
        queries = rotate(qkv[:, :D].reshape(SEQ, HEADS, HEAD_DIM), cos_table, sin_table).astype(jnp.bfloat16)
        key_vecs = rotate(qkv[:, D:2 * D].reshape(SEQ, HEADS, HEAD_DIM), cos_table, sin_table).astype(jnp.bfloat16)
        value_vecs = qkv[:, 2 * D:].reshape(SEQ, HEADS, HEAD_DIM).astype(jnp.bfloat16)
        return (queries, key_vecs, value_vecs)
    queries_all, keys_all, values_all = lax.map(front, (tok_blocks, phase_blocks))
    zero_block = jnp.zeros((1, SEQ, HEADS, HEAD_DIM), jnp.bfloat16)
    keys_prev = jnp.concatenate([zero_block, keys_all[:-1]], axis=0)
    values_prev = jnp.concatenate([zero_block, values_all[:-1]], axis=0)

    def middle(totals, inputs):
        tokens16, upstream16, queries, key_before, key_here, value_before, value_here, start_rows, block = inputs
        key_vecs = jnp.concatenate([key_before, key_here], axis=0)
        value_vecs = jnp.concatenate([value_before, value_here], axis=0)
        query_pos = block * SEQ + jnp.arange(SEQ, dtype=jnp.int32)
        key_pos = block * SEQ - SEQ + jnp.arange(2 * SEQ, dtype=jnp.int32)
        allowed = (key_pos[None, :] <= query_pos[:, None]) & (key_pos[None, :] >= start_rows[:, None])
        inputs_f, _, _, _, input_two = prepare(tokens16, pieces)
        mixed, log_total = attention_forward(queries, key_vecs, value_vecs, allowed)
        mixed_flat = mixed.reshape(SEQ, D)
        attn_out = jnp.dot(mixed_flat, mat_dense, preferred_element_type=jnp.float32) + bias_dense
        pre_up = jnp.dot(input_two, mat_up, preferred_element_type=jnp.float32) + bias_up
        active = gelu_exact(pre_up).astype(jnp.bfloat16)
        mlp_out = jnp.dot(active, mat_down, preferred_element_type=jnp.float32) + bias_down
        block_out = (inputs_f + attn_out + mlp_out).astype(jnp.bfloat16)
        down_sum = jnp.dot(active.T, upstream16, preferred_element_type=jnp.float32)
        grad_pre = jnp.dot(upstream16, mat_down.T, preferred_element_type=jnp.float32) * gelu_slope(pre_up)
        grad_pre16 = grad_pre.astype(jnp.bfloat16)
        up_sum = jnp.dot(input_two.T, grad_pre16, preferred_element_type=jnp.float32)
        grad_in_two = jnp.dot(grad_pre16, mat_up.T, preferred_element_type=jnp.float32)
        dense_sum = jnp.dot(mixed_flat.T, upstream16, preferred_element_type=jnp.float32)
        grad_mixed = jnp.dot(upstream16, mat_dense.T, preferred_element_type=jnp.float32).astype(jnp.bfloat16).reshape(SEQ, HEADS, HEAD_DIM)
        grad_query, grad_key, grad_value = attention_backward(queries, key_vecs, value_vecs, allowed, mixed, log_total, grad_mixed)
        totals = (totals[0] + dense_sum, totals[1] + up_sum, totals[2] + down_sum, totals[3] + lax.optimization_barrier(jnp.sum(grad_pre, axis=0)))
        return (totals, (block_out, grad_in_two, grad_query, grad_key, grad_value))
    middle_zeros = (jnp.zeros((D, D), jnp.float32), jnp.zeros((D, FF), jnp.float32), jnp.zeros((FF, D), jnp.float32), jnp.zeros((FF,), jnp.float32))
    middle_totals, (block_out, grad_two_all, grad_query_all, grad_key_win, grad_value_win) = lax.scan(middle, middle_zeros, (tok_blocks, up_blocks, queries_all, keys_prev, keys_all, values_prev, values_all, start_blocks, block_ids))
    zero_grad = jnp.zeros((1, SEQ, HEADS, HEAD_DIM), jnp.float32)
    own_key = grad_key_win[:, SEQ:] + jnp.concatenate([grad_key_win[1:, :SEQ], zero_grad], axis=0)
    own_value = grad_value_win[:, SEQ:] + jnp.concatenate([grad_value_win[1:, :SEQ], zero_grad], axis=0)

    def last(totals, inputs):
        tokens16, upstream16, phase_rows, grad_query, key_grad, value_grad, grad_in_two = inputs
        _, normed, scale_inv, input_one, _ = prepare(tokens16, pieces)
        cos_table, sin_table = rotary_tables(phase_rows)
        qkv_rows = jnp.concatenate([unrotate(grad_query, cos_table, sin_table).reshape(SEQ, D), unrotate(key_grad, cos_table, sin_table).reshape(SEQ, D), value_grad.reshape(SEQ, D)], axis=-1)
        qkv_rows16 = qkv_rows.astype(jnp.bfloat16)
        qkv_sum = jnp.dot(input_one.T, qkv_rows16, preferred_element_type=jnp.float32)
        grad_in_one = jnp.dot(qkv_rows16, mat_qkv.T, preferred_element_type=jnp.float32)
        back_one, gain_grad_one, bias_grad_one = norm_backward(grad_in_one, normed, scale_inv, gain_one)
        back_two, gain_grad_two, bias_grad_two = norm_backward(grad_in_two, normed, scale_inv, gain_two)
        upstream = upstream16.astype(jnp.float32)
        grad_tokens = upstream + back_one + back_two
        totals = (totals[0] + qkv_sum, totals[1] + gain_grad_one, totals[2] + bias_grad_one, totals[3] + gain_grad_two, totals[4] + bias_grad_two, totals[5] + lax.optimization_barrier(jnp.sum(qkv_rows, axis=0)), totals[6] + lax.optimization_barrier(jnp.sum(upstream, axis=0)))
        return (totals, grad_tokens)
    last_zeros = (jnp.zeros((D, 3 * D), jnp.float32), jnp.zeros((D,), jnp.float32), jnp.zeros((D,), jnp.float32), jnp.zeros((D,), jnp.float32), jnp.zeros((D,), jnp.float32), jnp.zeros((3 * D,), jnp.float32), jnp.zeros((D,), jnp.float32))
    last_totals, grad_tokens = lax.scan(last, last_zeros, (tok_blocks, up_blocks, phase_blocks, grad_query_all, own_key, own_value, grad_two_all))
    vector_sum = jnp.concatenate([last_totals[1], last_totals[2], last_totals[3], last_totals[4], last_totals[5], last_totals[6], middle_totals[3], last_totals[6]])
    sums = (last_totals[0], middle_totals[0], middle_totals[1], middle_totals[2], vector_sum)
    gradients = tuple((total / TOKENS for total in sums))
    firsts = (first_qkv, first_dense, first_up, first_down, first_vectors)
    seconds = (second_qkv, second_dense, second_up, second_down, second_vectors)
    rates = (rate_matrix, rate_matrix, rate_matrix, rate_matrix, rate_vector)
    updated = [adamw_update(masters[member], firsts[member], seconds[member], gradients[member], rates[member]) for member in range(5)]
    return (block_out.reshape(TOKENS, D), grad_tokens.reshape(TOKENS, D), gradients[0], gradients[1], gradients[2], gradients[3], gradients[4], updated[0][0], updated[1][0], updated[2][0], updated[3][0], updated[4][0], updated[0][1], updated[1][1], updated[2][1], updated[3][1], updated[4][1], updated[0][2], updated[1][2], updated[2][2], updated[3][2], updated[4][2])
```

```python
import jax
import jax.numpy as jnp
from jax import lax
from jax.experimental import pallas as pl
from jax.experimental.pallas import tpu as pltpu
from jax.sharding import PartitionSpec as P

HEADS = 12
HEAD_DIM = 64
ROTARY = 16
AXIS = "fsdp"

epsilon = 1e-05
rate_matrix = 0.05
rate_vector = 0.3
beta_one = 0.9
beta_two = 0.95
weight_decay = 0.01
adam_steps = 5
adam_floor = 1e-08
masked_score = -1e30
erf_scale = 0.7071067811865476
normal_density = 0.3989422804014327

bf16 = jnp.bfloat16
f32 = jnp.float32


def layer_norm(inputs):
    center = jnp.mean(inputs, axis=-1, keepdims=True)
    offset = inputs - center
    variance = jnp.mean(offset * offset, axis=-1, keepdims=True)
    scale_inv = lax.rsqrt(variance + epsilon)
    return (offset * scale_inv, scale_inv)


def norm_backward(upstream, normed, scale_inv, norm_gain):
    scaled = upstream * norm_gain
    projected = (
        scaled
        - jnp.mean(scaled, axis=-1, keepdims=True)
        - normed * jnp.mean(scaled * normed, axis=-1, keepdims=True)
    )
    return scale_inv * projected


def adamw_update(master, moment_one, moment_two, gradient, rate):
    moment_one = beta_one * moment_one + (1.0 - beta_one) * gradient
    moment_two = beta_two * moment_two + (1.0 - beta_two) * gradient * gradient
    corrected = (
        moment_one
        / (1.0 - beta_one**adam_steps)
        / (jnp.sqrt(moment_two / (1.0 - beta_two**adam_steps)) + adam_floor)
    )
    return (master - rate * (corrected + weight_decay * master), moment_one, moment_two)


def rotary_tables(phase):
    lane = jnp.arange(2 * HEAD_DIM) % HEAD_DIM
    half_dims = (lane % (ROTARY // 2)).astype(f32)
    frequency = jnp.exp(half_dims * (-2.0 * jnp.log(jnp.float32(10000.0)) / ROTARY))
    angles = phase[:, None] * jnp.where(lane < ROTARY, frequency, 0.0)[None, :]
    return jnp.cos(angles), jnp.sin(angles)


def rotate(values, cosines, sines, sign):
    span = ROTARY // 2
    width = values.shape[1]
    lane = lax.broadcasted_iota(jnp.int32, values.shape, 1) % HEAD_DIM
    ahead = pltpu.roll(values, width - span, 1)
    behind = pltpu.roll(values, span, 1)
    turned = jnp.where(lane < span, -ahead, behind)
    return values * cosines + (sign * sines) * turned


def attention_kernel(
    far_ref,
    x_ref,
    wq_ref,
    wk_ref,
    wv_ref,
    bq_ref,
    bk_ref,
    bv_ref,
    dense_ref,
    up_ref,
    cos_ref,
    sin_ref,
    phase_ref,
    mixed_ref,
    sq_ref,
    sk_ref,
    sv_ref,
    column_ref,
    back_ref,
    qs,
    gs,
    dq,
    kw,
    vw,
    dkw,
    dvw,
):
    step = pl.program_id(0)
    rows = up_ref.shape[0]
    half = rows // 2
    pair = 2 * HEAD_DIM
    lanes = lax.broadcasted_iota(jnp.int32, (half, pair), 1)
    contract = (((1,), (1,)), ((), ()))
    over_rows = (((0,), (0,)), ((), ()))

    def block(first, low, length):
        keys = kw[low : low + length, :]
        values = vw[low : low + length, :]
        query = qs[first : first + half, :] * jnp.asarray(0.125, bf16)
        upstream = gs[first : first + half, :]
        key_row = low + lax.broadcasted_iota(jnp.int32, (half, length), 1)
        query_row = 2 * rows + first + lax.broadcasted_iota(jnp.int32, (half, length), 0)
        begin = query_row - phase_ref[first : first + half, :]
        allowed = (key_row <= query_row) & (key_row >= begin)
        probs, queries, ups, parts = [], [], [], []
        for head in range(2):
            mask = (lanes // HEAD_DIM) == head
            masked_query = jnp.where(mask, query, jnp.zeros_like(query))
            scores = lax.dot_general(masked_query, keys, contract, preferred_element_type=f32)
            scores = jnp.where(allowed, scores, masked_score)
            highest = jnp.max(scores, axis=-1, keepdims=True)
            raised = jnp.exp(scores - highest)
            prob = raised * (1.0 / jnp.sum(raised, axis=-1, keepdims=True))
            prob_half = prob.astype(bf16)
            parts.append(jnp.dot(prob_half, values, preferred_element_type=f32))
            probs.append((prob, prob_half))
            queries.append(masked_query)
            ups.append(jnp.where(mask, upstream, jnp.zeros_like(upstream)))
        first_head = lanes < HEAD_DIM
        mixed = jnp.where(first_head, parts[0], parts[1]).astype(bf16)
        mixed_ref[first : first + half, :] = mixed
        wide = mixed.astype(f32)
        grads = []
        for head in range(2):
            prob, prob_half = probs[head]
            inner = jnp.sum(ups[head].astype(f32) * wide, axis=-1, keepdims=True)
            prob_grad = lax.dot_general(ups[head], values, contract, preferred_element_type=f32)
            score_grad = (prob * (prob_grad - inner)).astype(bf16)
            grads.append(jnp.dot(score_grad, keys, preferred_element_type=f32) * 0.125)
            dkw[low : low + length, :] += lax.dot_general(
                score_grad, queries[head], over_rows, preferred_element_type=f32
            )
            dvw[low : low + length, :] += lax.dot_general(
                prob_half, ups[head], over_rows, preferred_element_type=f32
            )
        dq[first : first + half, :] = jnp.where(first_head, grads[0], grads[1])

    def run(low, blocks):
        own = 2 * rows
        wq, wk, wv = wq_ref[...], wk_ref[...], wv_ref[...]
        seen = x_ref[low:, :]
        mine = x_ref[own:, :]
        cosines, sines = cos_ref[low:, :], sin_ref[low:, :]
        own_cos, own_sin = cos_ref[own:, :], sin_ref[own:, :]
        query = jnp.dot(mine, wq, preferred_element_type=f32) + bq_ref[...]
        qs[...] = rotate(query, own_cos, own_sin, 1.0).astype(bf16)
        key = jnp.dot(seen, wk, preferred_element_type=f32) + bk_ref[...]
        kw[low:, :] = rotate(key, cosines, sines, 1.0).astype(bf16)
        value = jnp.dot(seen, wv, preferred_element_type=f32) + bv_ref[...]
        vw[low:, :] = value.astype(bf16)
        gs[...] = lax.dot_general(
            up_ref[...], dense_ref[...], contract, preferred_element_type=f32
        ).astype(bf16)
        dkw[low:, :] = jnp.zeros((3 * rows - low, pair), f32)
        dvw[low:, :] = jnp.zeros((3 * rows - low, pair), f32)
        for item in blocks:
            block(*item)
        query_back = rotate(dq[...], own_cos, own_sin, -1.0)
        key_back = rotate(dkw[low:, :], cosines, sines, -1.0)
        value_back = dvw[low:, :]
        query16, key16 = query_back.astype(bf16), key_back.astype(bf16)
        value16 = value_back.astype(bf16)
        sums = [jnp.sum(part, axis=0, keepdims=True) for part in (query_back, key_back, value_back)]
        column_ref[...] = jnp.concatenate(sums + [jnp.zeros((5, pair), f32)], axis=0)
        sq_ref[...] = lax.dot_general(query16, mine, over_rows, preferred_element_type=f32).T
        sk_ref[...] = lax.dot_general(key16, seen, over_rows, preferred_element_type=f32).T
        sv_ref[...] = lax.dot_general(value16, seen, over_rows, preferred_element_type=f32).T

        @pl.when(step == 0)
        def _():
            back_ref[...] = jnp.zeros_like(back_ref)

        back_ref[low:, :] += lax.dot_general(
            key16, wk, contract, preferred_element_type=f32
        ) + lax.dot_general(value16, wv, contract, preferred_element_type=f32)
        back_ref[own:, :] += lax.dot_general(query16, wq, contract, preferred_element_type=f32)

    @pl.when(far_ref[0] == 0)
    def _():
        run(rows + half, ((0, rows + half, rows), (half, 2 * rows, rows)))

    @pl.when(far_ref[0] != 0)
    def _():
        run(0, ((0, 0, 2 * rows + half), (half, rows, 2 * rows)))


def attention(far, inputs, mat_qkv, bias, mat_dense, upstream, tables, phase):
    span, width = inputs.shape
    rows = upstream.shape[0]
    pair = 2 * HEAD_DIM
    half_width = mat_dense.shape[0]
    pairs = half_width // pair
    once = pl.Buffered(1)

    def fixed(shape):
        return pl.BlockSpec(shape, lambda i, far: (0, 0), pipeline_mode=once)

    def column(height, at):
        return pl.BlockSpec((height, pair), lambda i, far: (0, at * pairs + i))

    weights = [column(width, at) for at in range(3)]
    biases = [column(1, at) for at in range(3)]
    return pl.pallas_call(
        attention_kernel,
        grid_spec=pltpu.PrefetchScalarGridSpec(
            num_scalar_prefetch=1,
            grid=(pairs,),
            in_specs=[fixed((span, width))]
            + weights
            + biases
            + [pl.BlockSpec((pair, width), lambda i, far: (i, 0)), fixed((rows, width))]
            + [fixed((span, pair))] * 2
            + [fixed((rows, 1))],
            out_specs=[column(rows, 0)] + [column(width, 0)] * 3 + [column(8, 0)]
            + [pl.BlockSpec((span, width), lambda i, far: (0, 0))],
            scratch_shapes=[
                pltpu.VMEM((rows, pair), bf16),
                pltpu.VMEM((rows, pair), bf16),
                pltpu.VMEM((rows, pair), f32),
                pltpu.VMEM((span, pair), bf16),
                pltpu.VMEM((span, pair), bf16),
                pltpu.VMEM((span, pair), f32),
                pltpu.VMEM((span, pair), f32),
            ],
        ),
        out_shape=[jax.ShapeDtypeStruct((rows, half_width), bf16)]
        + [jax.ShapeDtypeStruct((width, half_width), f32)] * 3
        + [
            jax.ShapeDtypeStruct((8, half_width), f32),
            jax.ShapeDtypeStruct((span, width), f32),
        ],
        cost_estimate=pl.CostEstimate(
            flops=25_000_000_000, transcendentals=4_000_000, bytes_accessed=16_000_000
        ),
        compiler_params=pltpu.CompilerParams(
            dimension_semantics=("arbitrary",), vmem_limit_bytes=52 * 1024 * 1024
        ),
    )(far, inputs, mat_qkv, mat_qkv, mat_qkv, bias, bias, bias, mat_dense, upstream, *tables, phase)


def per_device(
    tokens,
    cotangent,
    segment_ids,
    weight_qkv,
    weight_dense,
    weight_up,
    weight_down,
    vectors,
    first_qkv,
    first_dense,
    first_up,
    first_down,
    first_vectors,
    second_qkv,
    second_dense,
    second_up,
    second_down,
    second_vectors,
):
    rows, width = tokens.shape
    hidden = weight_up.shape[1]
    devices = lax.axis_size(AXIS)
    device = lax.axis_index(AXIS)
    chips, layers = devices // 2, devices // 8
    chip, core = device // 2, device % 2
    level, y_at, x_at = chip // 4, (chip // 2) % 2, chip % 2
    total_tokens = rows * devices
    half_width, half_hidden = width // 2, hidden // 2
    shard = weight_qkv.shape[0]
    heads = HEADS // 2
    everyone = range(devices)

    def send(value, pairs):
        return lax.ppermute(value, AXIS, pairs)

    core_flip = [(d, d ^ 1) for d in everyone]
    x_flip = [(d, d ^ 2) for d in everyone]
    y_flip = [(d, d ^ 4) for d in everyone]

    def turn(steps):
        return [(d, (d + 8 * steps) % devices) for d in everyone]

    def later(steps, last=None):
        sources = devices - 2 * steps if last is None else last
        return [(d, d + 2 * steps) for d in range(sources)]

    def earlier(pairs):
        return [(b, a) for a, b in pairs]

    def pick(first, second):
        return (jnp.where(core == 0, first, second), jnp.where(core == 0, second, first))

    def after(value, *others):
        return lax.optimization_barrier((value, *others))[0]

    def by_rows(a, b):
        return lax.dot_general(a, b, (((0,), (0,)), ((), ())), preferred_element_type=f32)

    def by_columns(a, b):
        return lax.dot_general(a, b, (((1,), (1,)), ((), ())), preferred_element_type=f32)

    def row_of(value, at):
        return lax.dynamic_index_in_dim(value, at, 0, keepdims=False)

    def along(block):
        return [block] + [send(block, turn(s)) for s in range(1, layers)]

    def leveled(pieces):
        stacked = jnp.stack(pieces[::-1] + pieces[::-1])
        return lax.dynamic_slice_in_dim(stacked, layers - 1 - level, layers, 0)

    def around(mine, waits=()):
        from_x, from_y = send(mine, x_flip), send(mine, y_flip)
        cut = layers // 2
        via_x, via_y = after(from_x[:cut], *waits), after(from_y[cut:], *waits)
        across = jnp.concatenate([send(via_x, y_flip), send(via_y, x_flip)])
        return mine, from_x, from_y, across

    def settled(parts, low, high):
        mine, from_x, from_y, across = (part[..., low:high] for part in parts)
        here = [jnp.where(x_at == 0, mine, from_x), jnp.where(x_at == 0, from_x, mine)]
        there = [jnp.where(x_at == 0, from_y, across), jnp.where(x_at == 0, across, from_y)]
        picked = [jnp.where(y_at == 0, a, b) for a, b in zip(here, there)]
        other = [jnp.where(y_at == 0, b, a) for a, b in zip(here, there)]
        return jnp.stack(picked + other, axis=1).reshape(chips, -1, high - low)

    def collect(parts, travel=bf16):
        def block(y, x):
            stacks = [part.reshape(layers, 4, -1, part.shape[-1]) for part in parts]
            at = 2 * y + x
            return jnp.concatenate(
                [lax.dynamic_index_in_dim(s, at, 1, keepdims=False) for s in stacks], axis=-1
            )

        cut = layers // 2
        mine, to_x = block(y_at, x_at), block(y_at, 1 - x_at)
        to_y, across = block(1 - y_at, x_at), block(1 - y_at, 1 - x_at)
        across = across.astype(bf16)
        via_y, via_x = send(across[:cut], y_flip), send(across[cut:], x_flip)

        def plus(a, b):
            return (a.astype(f32) + b.astype(f32)).astype(bf16)

        from_x = send(jnp.concatenate([plus(to_x[:cut], via_y), to_x[cut:].astype(bf16)]), x_flip)
        from_y = send(jnp.concatenate([to_y[:cut].astype(bf16), plus(to_y[cut:], via_x)]), y_flip)
        sums = mine.astype(f32) + from_x.astype(f32) + from_y.astype(f32)
        result = row_of(sums, level)
        for steps in range(1, layers):
            out = row_of(sums, (level + steps) % layers).astype(travel)
            result = result + send(out, turn(steps)).astype(f32)
        return result

    qkv_cols = weight_qkv.astype(bf16).reshape(shard, 3, 2, half_width)
    qkv_cols = [qkv_cols[:, :, c].reshape(shard, 3 * half_width) for c in range(2)]
    up_cols = weight_up.astype(bf16).reshape(shard, chips, 2, half_hidden // chips)
    up_cols = [up_cols[:, :, c].reshape(shard, half_hidden) for c in range(2)]
    vec_lanes = vectors.shape[0] // shard
    vec16 = jnp.pad(vectors.astype(bf16).reshape(shard, vec_lanes), ((0, 0), (0, 128 - vec_lanes)))
    dense16 = weight_dense.astype(bf16)
    down16 = weight_down.astype(bf16)

    end = 3 * half_width
    keep, give = pick(*(jnp.concatenate([qkv_cols[c], up_cols[c]], axis=1) for c in range(2)))
    got = send(jnp.concatenate([give, vec16], axis=1), core_flip)
    both = jnp.concatenate(pick(jnp.concatenate([keep, vec16], axis=1), got))
    first_block = jnp.concatenate(
        [
            both[:, :end],
            jnp.concatenate([dense16[:, :half_width], dense16[:, half_width:]]),
            both[:, end + half_hidden :],
        ],
        axis=1,
    )
    up_block = both[:, end : end + half_hidden]
    down_rows = down16.shape[0] // 2
    down_block = jnp.concatenate([down16[:down_rows], down16[down_rows:]], axis=1)

    marks = jnp.pad(segment_ids.astype(bf16)[None], ((0, 15), (0, width - rows)))
    mine = jnp.concatenate([tokens, marks])
    near = send(mine, later(1))
    old = send(mine, later(2, 2))
    here = jnp.stack(pick(*(lambda v: (v, send(v, core_flip)))(jnp.concatenate([mine, cotangent]))))
    past = jnp.concatenate([old, near])
    past = jnp.stack(pick(past, send(past, core_flip)))
    tall = mine.shape[0]
    stretches = [past[:, :tall], past[:, tall:], here[:, :tall]]
    window = jnp.concatenate([part[:, :rows].reshape(2 * rows, width) for part in stretches])
    chip_up = here[:, tall:].reshape(2 * rows, width)
    numbers = [part[:, rows, :rows].reshape(-1).astype(f32) for part in stretches]
    numbers[0] = jnp.where(chip == 2, numbers[0], -1.0)
    numbers[1] = jnp.where(chip >= 1, numbers[1], -1.0)
    numbers = jnp.concatenate(numbers)
    places = jnp.arange(6 * rows)
    phase = jnp.sum(
        (numbers[None, :] == numbers[:, None]) & (places[None, :] < places[:, None]),
        axis=1,
        dtype=jnp.int32,
    )
    tables = rotary_tables(phase.astype(f32))
    normed, _ = layer_norm(window.astype(f32))

    level_one = leveled(along(first_block))
    turned = along(after(jnp.concatenate([up_block, down_block], axis=1), level_one))
    parts_one = around(level_one, (*tables, normed))
    parts_two = around(leveled([after(piece, *parts_one) for piece in turned]))

    mat_qkv = settled(parts_one, 0, end).reshape(width, end)
    dense_rows = settled(parts_one, end, end + half_width)
    dense_rows = jnp.concatenate([dense_rows[:, :shard], dense_rows[:, shard:]], axis=2)
    packed = settled(parts_one, end + half_width, end + half_width + 128)[:, :, :vec_lanes]
    packed = packed.reshape(-1).astype(f32)
    bounds = [0, 1, 2, 3, 4, 7, 8]
    bounds = [b * width for b in bounds] + [8 * width + hidden, 9 * width + hidden]
    pieces = [packed[bounds[i] : bounds[i + 1]] for i in range(8)]
    gain_one, bias_one, gain_two, bias_two, bias_qkv, bias_dense, bias_up, bias_down = pieces
    qkv_bias = row_of(jnp.moveaxis(bias_qkv.reshape(3, 2, half_width), 1, 0), core).reshape(-1)
    up_bias = row_of(jnp.moveaxis(bias_up.reshape(chips, 2, -1), 1, 0), core).reshape(-1)

    half_chips = chips // 2
    dense_keep = lax.dynamic_slice_in_dim(dense_rows, core * half_chips, half_chips, 0)
    dense_give = lax.dynamic_slice_in_dim(dense_rows, (1 - core) * half_chips, half_chips, 0)
    dense_pair = pick(dense_keep, send(dense_give, core_flip))
    mat_dense = jnp.stack(dense_pair, axis=1).reshape(half_width, width)

    input_one = (normed * gain_one + bias_one).astype(bf16)
    input_two = (normed[4 * rows :] * gain_two + bias_two).astype(bf16)

    far = ((chip == 1) | (chip == 2)).astype(jnp.int32).reshape(1)
    mixed, query_sum, key_sum, value_sum, column_sum, partial_one = attention(
        far,
        input_one,
        mat_qkv,
        qkv_bias[None],
        mat_dense,
        chip_up,
        tables,
        phase[4 * rows :, None],
    )

    mat_up = settled(parts_two, 0, half_hidden).reshape(width, half_hidden)
    down_pair = settled(parts_two, half_hidden, half_hidden + 2 * width)
    mat_down = jnp.concatenate([down_pair[..., :width], down_pair[..., width:]], axis=1)
    mat_down = mat_down.reshape(half_hidden, width)
    pre_up = jnp.dot(input_two, mat_up, preferred_element_type=f32) + up_bias
    gate = 0.5 * (1.0 + jax.scipy.special.erf(pre_up * erf_scale))
    active = (pre_up * gate).astype(bf16)
    slope = gate + pre_up * jnp.exp(-0.5 * pre_up * pre_up) * normal_density

    down_sum = by_rows(active, chip_up).astype(bf16)
    grad_pre = by_columns(chip_up, mat_down) * slope
    grad_pre16 = grad_pre.astype(bf16)
    up_sum = by_rows(input_two, grad_pre16).astype(bf16)
    dense_sum = by_rows(mixed, chip_up)
    def joined(partial):
        pairs = partial.reshape(-1, 2, rows, width)
        keep = lax.dynamic_index_in_dim(pairs, core, 1, keepdims=False)
        give = lax.dynamic_index_in_dim(pairs, 1 - core, 1, keepdims=False)
        return keep + send(give, core_flip)

    block_sum = joined(
        jnp.dot(mixed, mat_dense, preferred_element_type=f32)
        + jnp.dot(active, mat_down, preferred_element_type=f32)
    )[0]
    partial_two = by_columns(grad_pre16, mat_up)
    grad_in_two = joined(partial_two)[0]
    stretch_one = joined(partial_one)
    back_pairs = [(d, d - 2) for d in everyone if d >= 2 and (d % 2 == 1 or d < 6)]
    grad_in_one = (
        stretch_one[2]
        + send(stretch_one[1], back_pairs)
        + send(stretch_one[0], earlier(later(2, 2)))
    )
    own_inputs = tokens.astype(f32)
    block_out = (own_inputs + block_sum + (bias_dense + bias_down)).astype(bf16)
    own_normed, scale_inv = layer_norm(own_inputs)
    back_one = norm_backward(grad_in_one, own_normed, scale_inv, gain_one)
    back_two = norm_backward(grad_in_two, own_normed, scale_inv, gain_two)
    upstream = cotangent.astype(f32)
    grad_tokens = upstream + back_one + back_two

    dense_halves = dense_sum.reshape(half_chips, 2, shard, width)
    dense_halves = pick(dense_halves[:, 0], dense_halves[:, 1])
    dense_own = jnp.concatenate(pick(dense_halves[0], send(dense_halves[1], core_flip)))
    dense_own = jnp.concatenate([dense_own[..., :half_width], dense_own[..., half_width:]], axis=1)

    def only_mine(value):
        zero = jnp.zeros_like(value)
        return jnp.stack([jnp.where(core == 0, value, zero), jnp.where(core == 1, value, zero)], 1)

    output_sum = jnp.sum(upstream, axis=0)
    vector_sum = jnp.concatenate(
        [
            jnp.sum(partial_one * normed, axis=0),
            jnp.sum(partial_one, axis=0),
            jnp.sum(partial_two * normed[4 * rows :], axis=0),
            jnp.sum(partial_two, axis=0),
            only_mine(column_sum[:3]).reshape(-1),
            output_sum,
            only_mine(jnp.sum(grad_pre, axis=0).reshape(chips, -1)).reshape(-1),
            output_sum,
        ]
    )
    vector_part = jnp.pad(
        vector_sum.reshape(chips, 2 * shard, vec_lanes),
        ((0, 0), (0, 0), (0, 128 - vec_lanes)),
    )
    sum_one = collect(
        [part.reshape(chips, 2 * shard, half_width) for part in (query_sum, key_sum, value_sum)],
        f32,
    )
    down_parts = down_sum.reshape(chips, 2, down_rows, width)
    sum_down = collect([down_parts[:, 0], down_parts[:, 1], dense_own])
    sum_up = collect([up_sum.reshape(chips, 2 * shard, half_hidden), vector_part])

    def halves(value):
        keep = lax.dynamic_slice_in_dim(value, core * shard, shard, 0)
        give = lax.dynamic_slice_in_dim(value, (1 - core) * shard, shard, 0)
        return keep, send(give, core_flip)

    qkv_pair = pick(*halves(sum_one))
    up_keep, up_got = halves(sum_up)
    up_pair = pick(up_keep[:, :half_hidden], up_got[:, :half_hidden])
    factor = 1.0 / total_tokens
    grad_qkv = jnp.stack([part.reshape(shard, 3, half_width) for part in qkv_pair], axis=2)
    grad_up = jnp.stack([part.reshape(shard, chips, -1) for part in up_pair], axis=2)
    grad_vec = (up_keep + up_got)[:, half_hidden : half_hidden + vec_lanes].reshape(-1)
    dense_part = sum_down[:, 2 * width :]
    gradients = (
        grad_qkv.reshape(weight_qkv.shape) * factor,
        jnp.concatenate([dense_part[:shard], dense_part[shard:]], axis=1) * factor,
        grad_up.reshape(weight_up.shape) * factor,
        jnp.concatenate([sum_down[:, :width], sum_down[:, width : 2 * width]], axis=0) * factor,
        grad_vec * factor,
    )
    masters = (weight_qkv, weight_dense, weight_up, weight_down, vectors)
    firsts = (first_qkv, first_dense, first_up, first_down, first_vectors)
    seconds = (second_qkv, second_dense, second_up, second_down, second_vectors)
    rates = (rate_matrix, rate_matrix, rate_matrix, rate_matrix, rate_vector)
    updated = [
        adamw_update(
            masters[member], firsts[member], seconds[member], gradients[member], rates[member]
        )
        for member in range(5)
    ]
    return (
        block_out,
        grad_tokens,
        *gradients,
        *(member[0] for member in updated),
        *(member[1] for member in updated),
        *(member[2] for member in updated),
    )


def solution(mesh):
    matrix, vector = P(AXIS, None), P(AXIS)
    state = (matrix, matrix, matrix, matrix, vector)
    return jax.shard_map(
        per_device,
        mesh=mesh,
        in_specs=(matrix, matrix, vector, *state, *state, *state),
        out_specs=(matrix, matrix, *state, *state, *state, *state),
        check_vma=False,
    )
```

```python
import jax
import jax.numpy as jnp
from jax import lax
from jax.experimental import pallas as pl
from jax.experimental.pallas import tpu as pltpu
from jax.sharding import PartitionSpec as P

HEADS = 12
HEAD_DIM = 64
ROTARY = 16
AXIS = "fsdp"

epsilon = 1e-05
rate_matrix = 0.05
rate_vector = 0.3
beta_one = 0.9
beta_two = 0.95
weight_decay = 0.01
adam_steps = 5
adam_floor = 1e-08
masked_score = -1e30
erf_scale = 0.7071067811865476
normal_density = 0.3989422804014327

bf16 = jnp.bfloat16
f32 = jnp.float32


def layer_norm(inputs):
    center = jnp.mean(inputs, axis=-1, keepdims=True)
    offset = inputs - center
    variance = jnp.mean(offset * offset, axis=-1, keepdims=True)
    scale_inv = lax.rsqrt(variance + epsilon)
    return (offset * scale_inv, scale_inv)


def norm_backward(upstream, normed, scale_inv, norm_gain):
    scaled = upstream * norm_gain
    projected = (
        scaled
        - jnp.mean(scaled, axis=-1, keepdims=True)
        - normed * jnp.mean(scaled * normed, axis=-1, keepdims=True)
    )
    return scale_inv * projected


def adamw_update(master, moment_one, moment_two, gradient, rate):
    moment_one = beta_one * moment_one + (1.0 - beta_one) * gradient
    moment_two = beta_two * moment_two + (1.0 - beta_two) * gradient * gradient
    corrected = (
        moment_one
        / (1.0 - beta_one**adam_steps)
        / (jnp.sqrt(moment_two / (1.0 - beta_two**adam_steps)) + adam_floor)
    )
    return (master - rate * (corrected + weight_decay * master), moment_one, moment_two)


CONTRACT = (((1,), (1,)), ((), ()))
OVER_ROWS = (((0,), (0,)), ((), ()))


def by_columns(a, b):
    return lax.dot_general(a, b, CONTRACT, preferred_element_type=f32)


def by_rows(a, b):
    return lax.dot_general(a, b, OVER_ROWS, preferred_element_type=f32)


def rotate(values, cosines, sines, sign):
    span = ROTARY // 2
    width = values.shape[1]
    lane = lax.broadcasted_iota(jnp.int32, values.shape, 1) % HEAD_DIM
    ahead = pltpu.roll(values, width - span, 1)
    behind = pltpu.roll(values, span, 1)
    turned = jnp.where(lane < span, -ahead, behind)
    return values * cosines + (sign * sines) * turned


def each_chip(parts, place_ref, use):
    mine, from_x, from_y, low, high = parts
    layers, cut = mine.shape[0], low.shape[0]
    level, y_at, x_at = place_ref[2], place_ref[3], place_ref[4]
    for z in range(layers):
        slot = lax.rem(level - z + layers, layers)
        far = jnp.where(
            slot < cut, low[jnp.minimum(slot, cut - 1)], high[jnp.maximum(slot - cut, 0)]
        )
        a, b, c = mine[slot], from_x[slot], from_y[slot]
        for y in range(2):
            for x in range(2):
                near = jnp.where(x_at == x, a, b)
                other = jnp.where(x_at == x, c, far)
                use(4 * z + 2 * y + x, jnp.where(y_at == y, near, other))


def put(ways, chip, place_ref, value):
    z, y, x = chip // 4, (chip // 2) % 2, chip % 2
    way = jnp.where(place_ref[3] == y, 0, 2) + jnp.where(place_ref[4] == x, 0, 1)
    ways[way, z] = value.astype(ways.dtype)


def put_across(ways, low, high):
    cut = low.shape[0]
    low[...] = ways[3, :cut].astype(low.dtype)
    high[...] = ways[3, cut:].astype(high.dtype)


def attention_kernel(
    place_ref,
    mine_ref,
    from_x_ref,
    from_y_ref,
    low_ref,
    high_ref,
    tokens_ref,
    other_ref,
    up_ref,
    past_ref,
    other_past_ref,
    norms_ref,
    bias_ref,
    frequency_ref,
    attn_ref,
    second_ref,
    up_out_ref,
    normed_ref,
    sum_ref,
    sum_low_ref,
    sum_high_ref,
    dense_ref,
    column_ref,
    gain_ref,
    back,
    weights,
    window,
    inputs,
    numbers,
    queries,
    keys,
    values,
    ups,
    dqueries,
    dkeys,
    dvalues,
    mixes,
    phases,
):
    core = place_ref[1]
    rows = up_ref.shape[0]
    width = up_ref.shape[1]
    own = 4 * rows
    half_width = queries.shape[1]
    shard2 = mine_ref.shape[1]
    shard = shard2 // 2
    pair = 2 * HEAD_DIM
    mine_at = pl.multiple_of(core * rows, rows)
    other_at = pl.multiple_of((1 - core) * rows, rows)

    def weight(chip, value):
        weights[chip * shard2 : (chip + 1) * shard2, :] = value

    each_chip((mine_ref, from_x_ref, from_y_ref, low_ref, high_ref), place_ref, weight)

    tall = tokens_ref.shape[0]
    up_out_ref[pl.ds(mine_at, rows), :] = up_ref[...]
    up_out_ref[pl.ds(other_at, rows), :] = other_ref[tall : tall + rows, :]
    sources = (
        (past_ref, other_past_ref, 0, 0, place_ref[5]),
        (past_ref, other_past_ref, tall, 2 * rows, place_ref[6]),
        (tokens_ref, other_ref, 0, own, 1),
    )
    numbers[...] = jnp.zeros_like(numbers)
    for mine, other, first, at, there in sources:
        for ref, offset in ((mine, mine_at), (other, other_at)):
            window[pl.ds(pl.multiple_of(at + offset, rows), rows), :] = ref[
                first : first + rows, :
            ]
            mark = ref[first + rows : first + rows + 16, :rows].astype(f32)[:8]
            numbers[:, pl.ds(pl.multiple_of(at + offset, rows), rows)] = jnp.where(
                there == 1, mark, -1.0
            )

    def norm(at):
        center_in = window[at : at + rows, :].astype(f32)
        return layer_norm(center_in)[0]

    def block(first, low, length, at):
        lanes = lax.broadcasted_iota(jnp.int32, (rows, pair), 1)
        seen = (pl.ds(low, length), pl.ds(at, pair))
        asked = (pl.ds(first, rows), pl.ds(at, pair))
        key = keys[seen]
        value = values[seen]
        query = queries[asked] * jnp.asarray(0.125, bf16)
        upstream = ups[asked]
        phase = phases[pl.ds(first, rows), :]
        key_row = low + lax.broadcasted_iota(jnp.int32, (rows, length), 1)
        query_row = own + first + lax.broadcasted_iota(jnp.int32, (rows, length), 0)
        allowed = (key_row <= query_row) & (key_row >= query_row - phase)
        probs, masked_queries, masked_ups, parts = [], [], [], []
        for head in range(2):
            mask = (lanes // HEAD_DIM) == head
            masked_query = jnp.where(mask, query, jnp.zeros_like(query))
            scores = jnp.where(allowed, by_columns(masked_query, key), masked_score)
            highest = jnp.max(scores, axis=-1, keepdims=True)
            raised = jnp.exp(scores - highest)
            prob = raised * (1.0 / jnp.sum(raised, axis=-1, keepdims=True))
            prob_half = prob.astype(bf16)
            parts.append(jnp.dot(prob_half, value, preferred_element_type=f32))
            probs.append((prob, prob_half))
            masked_queries.append(masked_query)
            masked_ups.append(jnp.where(mask, upstream, jnp.zeros_like(upstream)))
        first_head = lanes < HEAD_DIM
        mixed = jnp.where(first_head, parts[0], parts[1]).astype(bf16)
        mixes[asked] = mixed
        wide = mixed.astype(f32)
        grads, key_parts, value_parts = [], [], []
        for head in range(2):
            prob, prob_half = probs[head]
            inner = jnp.sum(masked_ups[head].astype(f32) * wide, axis=-1, keepdims=True)
            score_grad = (prob * (by_columns(masked_ups[head], value) - inner)).astype(bf16)
            grads.append(jnp.dot(score_grad, key, preferred_element_type=f32) * 0.125)
            key_parts.append(by_rows(score_grad, masked_queries[head]))
            value_parts.append(by_rows(prob_half, masked_ups[head]))
        dkeys[seen] += key_parts[0] + key_parts[1]
        dvalues[seen] += value_parts[0] + value_parts[1]
        dqueries[asked] = jnp.where(first_head, grads[0], grads[1])

    def run(low, blocks):
        span = 6 * rows
        for at in range(low, span, rows):
            normed = norm(at)
            inputs[at : at + rows, :] = (normed * norms_ref[0:1, :] + norms_ref[1:2, :]).astype(bf16)
            if at >= own:
                normed_ref[at - own : at - own + rows, :] = normed
                second_ref[at - own : at - own + rows, :] = (
                    normed * norms_ref[2:3, :] + norms_ref[3:4, :]
                ).astype(bf16)
        number_row = numbers[0:1, :]
        number_column = jnp.transpose(numbers[...])[low:, 0:1]
        places = lax.broadcasted_iota(jnp.int32, (span - low, span), 1)
        here = low + lax.broadcasted_iota(jnp.int32, (span - low, span), 0)
        same = (number_row == number_column) & (places < here)
        phase = jnp.sum(jnp.where(same, 1.0, 0.0), axis=1, keepdims=True)
        angles = phase * frequency_ref[...]
        cosines, sines = jnp.cos(angles), jnp.sin(angles)
        own_cos, own_sin = cosines[own - low :], sines[own - low :]
        phases[...] = phase[own - low :].astype(jnp.int32)

        seen = inputs[low:, :]
        mine = inputs[own:, :]
        query = jnp.dot(mine, weights[:, :half_width], preferred_element_type=f32)
        query = query + bias_ref[0:1, :]
        key = jnp.dot(seen, weights[:, half_width : 2 * half_width], preferred_element_type=f32)
        key = key + bias_ref[1:2, :]
        value = jnp.dot(
            seen, weights[:, 2 * half_width : 3 * half_width], preferred_element_type=f32
        )
        values[low:, :] = (value + bias_ref[2:3, :]).astype(bf16)
        for at in range(0, half_width, pair):
            lanes = slice(at, at + pair)
            queries[:, lanes] = rotate(query[:, lanes], own_cos, own_sin, 1.0).astype(bf16)
            keys[low:, lanes] = rotate(key[:, lanes], cosines, sines, 1.0).astype(bf16)
        dense = weights[pl.ds(pl.multiple_of(core * half_width, half_width), half_width), 3 * half_width :]
        upstream = up_out_ref[...]
        ups[...] = by_columns(upstream, dense).astype(bf16)
        dkeys[low:, :] = jnp.zeros((span - low, half_width), f32)
        dvalues[low:, :] = jnp.zeros((span - low, half_width), f32)
        blocks()

        backs = []
        for at in range(0, half_width, pair):
            lanes = slice(at, at + pair)
            query_back = rotate(dqueries[:, lanes], own_cos, own_sin, -1.0)
            key_back = rotate(dkeys[low:, lanes], cosines, sines, -1.0)
            value_back = dvalues[low:, lanes]
            column_ref[:, lanes] = jnp.concatenate(
                [jnp.sum(part, axis=0, keepdims=True) for part in (query_back, key_back, value_back)]
                + [jnp.zeros((5, pair), f32)],
                axis=0,
            )
            backs.append([part.astype(bf16) for part in (query_back, key_back, value_back)])
        query16, key16, value16 = (
            jnp.concatenate([part[i] for part in backs], axis=1) for i in range(3)
        )
        both16 = jnp.concatenate([key16, value16], axis=1)
        result = jnp.concatenate([by_rows(mine, query16), by_rows(seen, both16)], axis=1)
        for chip in range(width // shard2):
            put(sum_ref, chip, place_ref, result[chip * shard2 : (chip + 1) * shard2, :])
        put_across(sum_ref, sum_low_ref, sum_high_ref)
        gain = jnp.zeros((1, width), f32)
        plain = jnp.zeros((1, width), f32)
        for at in range(0, span, rows):
            whose = jnp.where(core == (at // rows) % 2, 0, 1)
            if at < low:
                back[whose, at // (2 * rows)] = jnp.zeros((rows, width), f32)
                continue
            part = by_columns(both16[at - low : at - low + rows], weights[:, half_width : 3 * half_width])
            if at >= own:
                part = part + by_columns(query16[at - own : at - own + rows], weights[:, :half_width])
            back[whose, at // (2 * rows)] = part
            gain = gain + jnp.sum(part * norm(at), axis=0, keepdims=True)
            plain = plain + jnp.sum(part, axis=0, keepdims=True)
        gain_ref[...] = jnp.concatenate([gain, plain, jnp.zeros((6, width), f32)], axis=0)
        mixed = mixes[...]
        attn_ref[...] = jnp.dot(mixed, dense, preferred_element_type=f32)
        result = by_rows(mixed, upstream)
        for device in range(half_width // shard):
            whose = jnp.where(core == device % 2, 0, 1)
            part = result[device * shard : (device + 1) * shard, :]
            dense_ref[whose, device // 2] = part.astype(bf16)

    @pl.when(place_ref[0] == 0)
    def _():
        def blocks():
            def turn(i, carry):
                at = pl.multiple_of((i // 2) * pair, pair)
                first = pl.multiple_of((i % 2) * rows, rows)
                block(first, pl.multiple_of(first + 3 * rows, rows), 2 * rows, at)
                return carry

            lax.fori_loop(0, 2 * (half_width // pair), turn, 0)

        run(3 * rows, blocks)

    @pl.when(place_ref[0] != 0)
    def _():
        def blocks():
            def turn(i, carry):
                at = pl.multiple_of(i * pair, pair)
                block(0, 0, 5 * rows, at)
                block(rows, 2 * rows, 4 * rows, at)
                return carry

            lax.fori_loop(0, half_width // pair, turn, 0)

        run(0, blocks)


def whole(count):
    return [pl.BlockSpec(memory_space=pltpu.VMEM)] * count


def attention(place, parts, tokens, other, upstream, past, other_past, norms, bias, frequency):
    layers, shard2, wide = parts[0].shape
    rows, width = upstream.shape
    half_width = bias.shape[1]
    chips = 4 * layers
    span = 6 * rows
    block = (shard2, 3 * half_width)
    out_shape = [
        ((2 * rows, width), f32),
        ((2 * rows, width), bf16),
        ((2 * rows, width), bf16),
        ((2 * rows, width), f32),
        ((4, layers, *block), f32),
        ((layers // 2, *block), bf16),
        ((layers - layers // 2, *block), bf16),
        ((2, chips // 2, shard2 // 2, width), bf16),
        ((8, half_width), f32),
        ((8, width), f32),
        ((2, 3, rows, width), f32),
    ]
    scratch = [
        ((width, wide), bf16),
        ((span, width), bf16),
        ((span, width), bf16),
        ((8, span), f32),
        ((2 * rows, half_width), bf16),
        ((span, half_width), bf16),
        ((span, half_width), bf16),
        ((2 * rows, half_width), bf16),
        ((2 * rows, half_width), f32),
        ((span, half_width), f32),
        ((span, half_width), f32),
        ((2 * rows, half_width), bf16),
        ((2 * rows, 1), jnp.int32),
    ]
    return pl.pallas_call(
        attention_kernel,
        in_specs=[pl.BlockSpec(memory_space=pltpu.SMEM)] + whole(13),
        out_specs=whole(11),
        out_shape=[jax.ShapeDtypeStruct(shape, kind) for shape, kind in out_shape],
        scratch_shapes=[pltpu.VMEM(shape, kind) for shape, kind in scratch],
        cost_estimate=pl.CostEstimate(
            flops=25_000_000_000, transcendentals=4_000_000, bytes_accessed=16_000_000
        ),
        compiler_params=pltpu.CompilerParams(vmem_limit_bytes=58 * 1024 * 1024),
    )(place, *parts, tokens, other, upstream, past, other_past, norms, bias, frequency)


def feed_forward_kernel(
    place_ref,
    mine_ref,
    from_x_ref,
    from_y_ref,
    low_ref,
    high_ref,
    second_ref,
    up_ref,
    normed_ref,
    attn_ref,
    bias_ref,
    dense_ref,
    other_dense_ref,
    out_keep_ref,
    out_give_ref,
    back_keep_ref,
    back_give_ref,
    wide_ref,
    wide_low_ref,
    wide_high_ref,
    hidden_ref,
    gain_ref,
    mat_up,
    mat_down,
    total,
):
    core = place_ref[1]
    double, width = second_ref.shape
    rows = double // 2
    shard2 = mine_ref.shape[1]
    shard = shard2 // 2
    chips = width // shard2
    hidden = mat_up.shape[1]
    down_rows = mat_down.shape[0] // chips
    half = down_rows // 2

    def weight(chip, value):
        mat_up[chip * shard2 : (chip + 1) * shard2, :] = value[:, :hidden]
        at = chip * down_rows
        mat_down[at : at + half, :] = value[:, hidden : hidden + width]
        mat_down[at + half : at + down_rows, :] = value[:, hidden + width :]

    each_chip((mine_ref, from_x_ref, from_y_ref, low_ref, high_ref), place_ref, weight)
    second, upstream = second_ref[...], up_ref[...]
    pre_up = jnp.dot(second, mat_up[...], preferred_element_type=f32) + bias_ref[...]
    gate = 0.5 * (1.0 + lax.erf(pre_up * erf_scale))
    active = (pre_up * gate).astype(bf16)
    slope = gate + pre_up * jnp.exp(-0.5 * pre_up * pre_up) * normal_density
    grad_pre = by_columns(upstream, mat_down[...]) * slope
    grad_pre16 = grad_pre.astype(bf16)
    hidden_ref[...] = jnp.concatenate(
        [jnp.sum(grad_pre, axis=0, keepdims=True), jnp.zeros((7, hidden), f32)], axis=0
    )
    down_sum = by_rows(active, upstream).astype(bf16)
    up_sum = by_rows(second, grad_pre16).astype(bf16)
    for chip in range(chips):
        at = chip * down_rows
        i = chip % (chips // 2)
        ours = core == (0 if chip < chips // 2 else 1)
        dense = jnp.where(ours, dense_ref[i].astype(f32), other_dense_ref[i].astype(f32))
        dense = jnp.concatenate([dense[:, : width // 2], dense[:, width // 2 :]], axis=0)
        pieces = [down_sum[at : at + half, :], down_sum[at + half : at + down_rows, :]]
        pieces = pieces + [dense.astype(bf16), up_sum[chip * shard2 : (chip + 1) * shard2, :]]
        put(wide_ref, chip, place_ref, jnp.concatenate(pieces, axis=1))
    put_across(wide_ref, wide_low_ref, wide_high_ref)
    mine_at = pl.multiple_of(core * rows, rows)
    other_at = pl.multiple_of((1 - core) * rows, rows)
    total[...] = attn_ref[...] + jnp.dot(active, mat_down[...], preferred_element_type=f32)
    out_keep_ref[...] = total[pl.ds(mine_at, rows), :]
    out_give_ref[...] = total[pl.ds(other_at, rows), :]
    back = by_columns(grad_pre16, mat_up[...])
    gain_ref[...] = jnp.concatenate(
        [
            jnp.sum(back * normed_ref[...], axis=0, keepdims=True),
            jnp.sum(back, axis=0, keepdims=True),
            jnp.zeros((6, width), f32),
        ],
        axis=0,
    )
    total[...] = back
    back_keep_ref[...] = total[pl.ds(mine_at, rows), :]
    back_give_ref[...] = total[pl.ds(other_at, rows), :]


def feed_forward(place, parts, second, upstream, normed, attn, bias, dense, other_dense):
    layers, shard2, _ = parts[0].shape
    double, width = second.shape
    hidden = bias.shape[1]
    chips = 4 * layers
    wide = 2 * width + width // 2
    share = ((double // 2, width), f32)
    block = (shard2, wide + hidden)
    out_shape = (
        [share] * 4
        + [((4, layers, *block), bf16)]
        + [((layers // 2, *block), bf16), ((layers - layers // 2, *block), bf16)]
        + [((8, hidden), f32), ((8, width), f32)]
    )
    scratch = [
        ((width, hidden), bf16),
        ((hidden, width), bf16),
        ((double, width), f32),
    ]
    return pl.pallas_call(
        feed_forward_kernel,
        in_specs=[pl.BlockSpec(memory_space=pltpu.SMEM)] + whole(12),
        out_specs=whole(9),
        out_shape=[jax.ShapeDtypeStruct(shape, kind) for shape, kind in out_shape],
        scratch_shapes=[pltpu.VMEM(shape, kind) for shape, kind in scratch],
        cost_estimate=pl.CostEstimate(
            flops=12_000_000_000, transcendentals=2_000_000, bytes_accessed=20_000_000
        ),
        compiler_params=pltpu.CompilerParams(vmem_limit_bytes=58 * 1024 * 1024),
    )(place, *parts, second, upstream, normed, attn, bias, dense, other_dense)


def per_device(
    tokens,
    cotangent,
    segment_ids,
    weight_qkv,
    weight_dense,
    weight_up,
    weight_down,
    vectors,
    first_qkv,
    first_dense,
    first_up,
    first_down,
    first_vectors,
    second_qkv,
    second_dense,
    second_up,
    second_down,
    second_vectors,
):
    rows, width = tokens.shape
    hidden = weight_up.shape[1]
    devices = lax.axis_size(AXIS)
    device = lax.axis_index(AXIS)
    chips, layers = devices // 2, devices // 8
    chip, core = device // 2, device % 2
    level, y_at, x_at = chip // 4, (chip // 2) % 2, chip % 2
    total_tokens = rows * devices
    half_width, half_hidden = width // 2, hidden // 2
    shard = weight_qkv.shape[0]
    everyone = range(devices)

    def send(value, pairs):
        return lax.ppermute(value, AXIS, pairs)

    core_flip = [(d, d ^ 1) for d in everyone]
    x_flip = [(d, d ^ 2) for d in everyone]
    y_flip = [(d, d ^ 4) for d in everyone]

    def turn(steps):
        return [(d, (d + 8 * steps) % devices) for d in everyone]

    def later(steps, last=None):
        sources = devices - 2 * steps if last is None else last
        return [(d, d + 2 * steps) for d in range(sources)]

    def earlier(pairs):
        return [(b, a) for a, b in pairs]

    def pick(first, second):
        return (jnp.where(core == 0, first, second), jnp.where(core == 0, second, first))

    def after(value, *others):
        return lax.optimization_barrier((value, *others))[0]

    def row_of(value, at):
        return lax.dynamic_index_in_dim(value, at, 0, keepdims=False)

    place = jnp.stack(
        [
            ((chip == 1) | (chip == 2)).astype(jnp.int32),
            core,
            level,
            y_at,
            x_at,
            (chip == 2).astype(jnp.int32),
            (chip >= 1).astype(jnp.int32),
            jnp.int32(0),
        ]
    ).astype(jnp.int32)
    cut = layers // 2

    def along(block):
        return [block] + [send(block, turn(s)) for s in range(1, layers)]

    def first_hop(pieces):
        mine = jnp.stack(pieces)
        return mine, send(mine, x_flip), send(mine, y_flip)

    def second_hop(mine, from_x, from_y, *waits):
        via_x, via_y = after(from_x[:cut], *waits), after(from_y[cut:], *waits)
        return mine, from_x, from_y, send(via_x, y_flip), send(via_y, x_flip)

    def starts(ways, low, high):
        return ways, send(low, y_flip), send(high, x_flip)

    def falls(hop, waits=()):
        ways, via_y, via_x = hop
        mine, to_x, to_y = ways[0], ways[1], ways[2]
        if waits:
            via_y, via_x = after(via_y, *waits), after(via_x, *waits)

        def plus(a, b):
            return (a.astype(f32) + b.astype(f32)).astype(bf16)

        from_x = send(jnp.concatenate([plus(to_x[:cut], via_y), to_x[cut:].astype(bf16)]), x_flip)
        from_y = send(jnp.concatenate([to_y[:cut].astype(bf16), plus(to_y[cut:], via_x)]), y_flip)
        return mine, from_x, from_y

    def rises(hop, travel=bf16):
        mine, from_x, from_y = hop
        sums = mine.astype(f32) + from_x.astype(f32) + from_y.astype(f32)
        arrived = [row_of(sums, level)]
        for steps in range(1, layers):
            out = row_of(sums, (level + steps) % layers).astype(travel)
            arrived.append(send(out, turn(steps)))
        return arrived

    def settle(arrived):
        result = arrived[0]
        for part in arrived[1:]:
            result = result + part.astype(f32)
        return result

    end = 3 * half_width
    qkv_cols = weight_qkv.astype(bf16).reshape(shard, 3, 2, half_width)
    qkv_cols = [qkv_cols[:, :, c].reshape(shard, end) for c in range(2)]
    up_cols = weight_up.astype(bf16).reshape(shard, chips, 2, half_hidden // chips)
    up_cols = [up_cols[:, :, c].reshape(shard, half_hidden) for c in range(2)]
    dense16 = weight_dense.astype(bf16)
    down16 = weight_down.astype(bf16)
    keep, give = pick(*(jnp.concatenate([qkv_cols[c], up_cols[c]], axis=1) for c in range(2)))
    got = send(jnp.concatenate([give, dense16], axis=1), core_flip)
    both = jnp.concatenate(pick(jnp.concatenate([keep, dense16], axis=1), got))
    first_block = jnp.concatenate([both[:, :end], both[:, end + half_hidden :]], axis=1)
    up_block = both[:, end : end + half_hidden]
    down_rows = down16.shape[0] // 2
    down_block = jnp.concatenate([down16[:down_rows], down16[down_rows:]], axis=1)

    mine_vec = vectors.shape[0]
    vector_rows = -(-devices * mine_vec // 1024) * 8

    def added(block):
        every = lax.all_gather(block.reshape(vector_rows, 128), AXIS, axis=0, tiled=True)
        return jnp.sum(every.reshape(devices, vector_rows, 128), axis=0).reshape(-1)

    placed = lax.dynamic_update_slice_in_dim(
        jnp.zeros((vector_rows * 128,), f32),
        lax.reduce_precision(vectors, 8, 7),
        device * mine_vec,
        0,
    )
    packed = added(placed)
    bounds = [0, 1, 2, 3, 4, 7, 8]
    bounds = [b * width for b in bounds] + [8 * width + hidden, 9 * width + hidden]
    pieces = [packed[bounds[i] : bounds[i + 1]] for i in range(8)]
    gain_one, bias_one, gain_two, bias_two, bias_qkv, bias_dense, bias_up, bias_down = pieces
    norms = packed[: 4 * width].reshape(4, width)
    qkv_bias = row_of(jnp.moveaxis(bias_qkv.reshape(3, 2, half_width), 1, 0), core)
    up_bias = row_of(jnp.moveaxis(bias_up.reshape(chips, 2, -1), 1, 0), core).reshape(1, -1)

    marks = jnp.pad(segment_ids.astype(bf16)[None], ((0, 15), (0, width - rows)))
    mine = jnp.concatenate([tokens, marks])
    near = send(mine, later(1))
    old = send(mine, later(2, 2))
    other = send(jnp.concatenate([mine, cotangent]), core_flip)
    past = jnp.concatenate([old, near])
    other_past = send(past, core_flip)
    lane = jnp.arange(2 * HEAD_DIM) % HEAD_DIM
    half_dims = (lane % (ROTARY // 2)).astype(f32)
    frequency = jnp.exp(half_dims * (-2.0 * jnp.log(jnp.float32(10000.0)) / ROTARY))
    frequency = jnp.where(lane < ROTARY, frequency, 0.0)[None]

    pieces_one = along(first_block)
    pieces_up = along(after(up_block, *pieces_one))
    hop_one = first_hop(pieces_one)
    pieces_down = along(after(down_block, *pieces_up, *hop_one))
    parts_one = second_hop(*hop_one, *pieces_up)
    pieces_two = [jnp.concatenate(pair, axis=1) for pair in zip(pieces_up, pieces_down)]
    hop_two = first_hop([after(piece, parts_one[3], parts_one[4]) for piece in pieces_two])
    parts_two = second_hop(*hop_two)

    (
        attn,
        second,
        chip_up,
        chip_normed,
        *qkv_sums,
        dense_sums,
        column_sum,
        gain_sum_one,
        back,
    ) = attention(
        place,
        parts_one,
        mine,
        other,
        cotangent,
        after(past, hop_two[0]),
        other_past,
        norms,
        qkv_bias,
        frequency,
    )
    one_hop = falls(starts(*qkv_sums), parts_two[3:])
    dense_got = send(dense_sums[1], core_flip)
    (
        out_keep,
        out_give,
        two_keep,
        two_give,
        *wide_sums,
        hidden_sum,
        gain_sum_two,
    ) = feed_forward(
        place, parts_two, second, chip_up, chip_normed, attn, up_bias, dense_sums[0], dense_got
    )
    sum_one_parts = rises(one_hop, f32)

    upstream = cotangent.astype(f32)

    def only_mine(value):
        zero = jnp.zeros_like(value)
        return jnp.stack([jnp.where(core == 0, value, zero), jnp.where(core == 1, value, zero)], 1)

    output_sum = jnp.sum(upstream, axis=0)
    vector_sum = jnp.concatenate(
        [
            gain_sum_one[:2].reshape(-1),
            gain_sum_two[:2].reshape(-1),
            only_mine(column_sum[:3]).reshape(-1),
            output_sum,
            only_mine(hidden_sum[0].reshape(chips, -1)).reshape(-1),
            output_sum,
        ]
    )
    vector_block = jnp.pad(vector_sum, (0, vector_rows * 128 - vector_sum.shape[0]))
    wide_hop = starts(wide_sums[0], *(after(part, vector_block) for part in wide_sums[1:]))
    wide_hop = falls(wide_hop)
    sum_one = settle(sum_one_parts)
    grad_vec = lax.dynamic_slice_in_dim(added(vector_block), device * mine_vec, mine_vec, 0)

    back = after(back, *sum_one_parts[1:])
    stretch_one = back[0] + send(back[1], core_flip)
    back_pairs = [(d, d - 2) for d in everyone if d >= 2 and (d % 2 == 1 or d < 6)]
    back_near = send(after(stretch_one[1], *wide_hop[1:]), back_pairs)
    back_old = send(after(stretch_one[0], *wide_hop[1:]), earlier(later(2, 2)))
    grad_in_one = stretch_one[2] + back_near + back_old
    wide_hop = (after(wide_hop[0], *sum_one_parts[1:]), *wide_hop[1:])
    wide_parts = rises(wide_hop)
    wide_parts[0] = after(wide_parts[0], back_near, back_old)
    sum_wide = settle(wide_parts)
    own_inputs = tokens.astype(f32)
    block_sum = out_keep + send(out_give, core_flip)
    grad_in_two = two_keep + send(two_give, core_flip)
    block_out = (own_inputs + block_sum + (bias_dense + bias_down)).astype(bf16)
    own_normed, scale_inv = layer_norm(own_inputs)
    back_one = norm_backward(grad_in_one, own_normed, scale_inv, gain_one)
    back_two = norm_backward(grad_in_two, own_normed, scale_inv, gain_two)
    grad_tokens = upstream + back_one + back_two

    def halves(value):
        keep = lax.dynamic_slice_in_dim(value, core * shard, shard, 0)
        give = lax.dynamic_slice_in_dim(value, (1 - core) * shard, shard, 0)
        return keep, send(give, core_flip)

    qkv_pair = pick(*halves(sum_one))
    up_pair = pick(*halves(sum_wide[:, 2 * width + half_width :]))
    sum_down = sum_wide[:, : 2 * width + half_width]
    factor = 1.0 / total_tokens
    grad_qkv = jnp.stack([part.reshape(shard, 3, half_width) for part in qkv_pair], axis=2)
    grad_up = jnp.stack([part.reshape(shard, chips, -1) for part in up_pair], axis=2)
    grad_qkv = after(grad_qkv.reshape(weight_qkv.shape))
    grad_up = after(grad_up.reshape(weight_up.shape))
    dense_part = sum_down[:, 2 * width :]
    gradients = (
        grad_qkv.reshape(weight_qkv.shape) * factor,
        jnp.concatenate([dense_part[:shard], dense_part[shard:]], axis=1) * factor,
        grad_up.reshape(weight_up.shape) * factor,
        jnp.concatenate([sum_down[:, :width], sum_down[:, width : 2 * width]], axis=0) * factor,
        grad_vec * factor,
    )
    masters = (weight_qkv, weight_dense, weight_up, weight_down, vectors)
    firsts = (first_qkv, first_dense, first_up, first_down, first_vectors)
    seconds = (second_qkv, second_dense, second_up, second_down, second_vectors)
    rates = (rate_matrix, rate_matrix, rate_matrix, rate_matrix, rate_vector)
    updated = [
        adamw_update(
            masters[member], firsts[member], seconds[member], gradients[member], rates[member]
        )
        for member in range(5)
    ]
    return (
        block_out,
        grad_tokens,
        *gradients,
        *(member[0] for member in updated),
        *(member[1] for member in updated),
        *(member[2] for member in updated),
    )


def solution(mesh):
    matrix, vector = P(AXIS, None), P(AXIS)
    state = (matrix, matrix, matrix, matrix, vector)
    return jax.shard_map(
        per_device,
        mesh=mesh,
        in_specs=(matrix, matrix, vector, *state, *state, *state),
        out_specs=(matrix, matrix, *state, *state, *state, *state),
        check_vma=False,
    )
```
